32 devices in a mesh: groups: 2 (over x), patch: 8 (over z, y), section: 2 (over core).
Axes of the slice: x: 2, y: 2, z: 4, core: 2. Of those that a mesh axis runs over, the one named last changes fastest.
Arguments:
- hidden_in: bfloat16 [6144, 3072], P(('groups', 'patch')), parts along dimension 0, may hold values from -6 to 6
- text_rows: bfloat16 [256, 3072], P('groups', 'patch'), parts along dimension 0, may hold values from -6 to 6
- mod_table: float32 [50, 2, 5, 3072], P(None, 'section'), may hold values from -3 to 3
- timestep: int32 [2], P('groups'), parts along dimension 0, may hold values from 0 to 49
- w_query: bfloat16 [2, 3072, 1536], P('section', 'patch'), may hold values from -0.109375 to 0.109375
- w_out: bfloat16 [2, 1536, 3072], P('section', 'patch'), may hold values from -1.25 to 1.25
- w_text: bfloat16 [2, 3072, 3072], P('section', 'patch'), may hold values from -0.109375 to 0.109375
- stale_kv: bfloat16 [2, 6144, 3072], P('section', ('groups', 'patch')), parts along dimension 1, may hold values from -450 to 450
- mask_blocks: int32 [48, 4], P(('groups', 'patch')), parts along dimension 0, may hold values from 0 to 23, as said below
- counts: int32 [48], P(('groups', 'patch')), parts along dimension 0, may hold values from 1 to 4, as said below
Outputs:
- hidden_out: bfloat16 [2, 6144, 3072], P('section', ('groups', 'patch')), parts along dimension 1
The draws below stay inside these ranges and needn't reach their ends.
There are 2 independent parts, one for each index of `groups`. The reference program is written for one: setup_inputs(seed, part) draws one part's arguments, and reference() takes and returns one part's arrays. A program takes and returns all parts, laid end to end along the dimension named above; an argument that names none is the same for every part. Nothing has to cross between parts.
Inputs may be any that keep to these rules, and one draw needn't show every extreme that they name: `mask_blocks`: row b lists 4 different block numbers, b itself first; every one is a block stored on the same patch device as block b or on the device just before or after it (384 tokens a device, blocks of 128 tokens). Only the first counts[b] entries of row b of mask_blocks are used; some block has 4.
All inputs are finite; a program needn't handle non-finite values.
Results may differ from the reference program's by a relative error of at most 0.037.
Values may be sent and summed in bfloat16 or wider, within the bound.
A program may use at most 128 MiB of HBM per device.

```python
import jax
import jax.numpy as jnp
from jax import lax

D = 3072
HEADS = 12
HD = 128
INNER = 1536
BLK = 128
WIN = 4
TXT = 128
STEPS = 50
TOK_DEV = 384
SEQ = 3072
NBLK = 24
LAYERS = 2


def draw_mask_blocks(key, part):
    per_device = TOK_DEV // BLK
    span = 3 * per_device
    block = jnp.arange(NBLK, dtype=jnp.int32)
    home = block // per_device
    offsets = jnp.arange(span, dtype=jnp.int32)
    candidate = (home[:, None] - 1) * per_device + offsets[None, :]
    usable = (candidate >= 0) & (candidate < NBLK) & (candidate != block[:, None])
    noise = jax.random.randint(jax.random.fold_in(key, 7), (NBLK, span), 0, 1 << 18)
    score = jnp.where(usable, noise * span + offsets[None, :], (1 << 30) + offsets[None, :])
    order = jnp.argsort(score, axis=1, stable=True)
    picked = jnp.take_along_axis(candidate, order[:, :WIN - 1], axis=1)
    return jnp.concatenate([block[:, None], picked], axis=1).astype(jnp.int32)


def draw_counts(key, part):
    base = jax.random.randint(jax.random.fold_in(key, 13), (NBLK,), 1, WIN + 1)
    filled = jax.random.randint(jax.random.fold_in(key, 17), (), 0, NBLK)
    return jnp.where(jnp.arange(NBLK) == filled, WIN, base).astype(jnp.int32)


def draw_stale_kv(key, part):
    shape = (LAYERS, SEQ, 2 * INNER)
    base = jax.random.normal(jax.random.fold_in(key, 3), shape, jnp.float32)
    return jnp.clip(base, -6.0, 6.0).astype(jnp.bfloat16)


def levels(own_key, dims, split, least, top_value):
    factor_of, own = 1.0, jax.random.fold_in(own_key, 6)
    for dim, parts in split:
        draws = jnp.exp(jax.random.uniform(jax.random.fold_in(own, dim), (parts,), jnp.float32, least / len(split), top_value / len(split)))
        factor_of = factor_of * jnp.repeat(draws, dims[dim] // parts).reshape([-1 if axis == dim else 1 for axis in range(len(dims))])
    return factor_of


def scatter_about(rng, dims, deviation, bound, cuts=(), kind=jnp.bfloat16):
    loudness = levels(rng, dims, cuts, -0.22, 0.18) if cuts else 1.0
    drawn = jax.random.normal(rng, dims, jnp.float32) * deviation * loudness
    return jnp.minimum(jnp.maximum(drawn, -bound), bound).astype(kind)


def setup_inputs(seed: int = 0, part: int = 0) -> dict:
    splits = jax.random.split(jax.random.key(seed), 11)
    part_keys = jax.random.split(jax.random.fold_in(splits[10], part), 11)
    hidden_in = scatter_about(part_keys[0], (SEQ, D), 1.0, 6.0, ((0, 8),))
    text_rows = scatter_about(part_keys[1], (TXT, D), 1.0, 6.0, ((1, 8),))
    mod_table = scatter_about(splits[2], (STEPS, LAYERS, 5, D), 0.5, 3.0, ((1, 2),), jnp.float32)
    timestep = jax.random.randint(part_keys[3], (1,), 0, STEPS).astype(jnp.int32)
    w_query = scatter_about(splits[4], (LAYERS, D, INNER), D ** -0.5, 0.109375, ((0, 2), (1, 8)))
    w_out = scatter_about(splits[5], (LAYERS, INNER, D), (max(INNER // 64, 1)) ** -0.5, 1.25, ((0, 2), (1, 8)))
    w_text = scatter_about(splits[6], (LAYERS, D, 2 * INNER), D ** -0.5, 0.109375, ((0, 2), (1, 8)))
    stale_kv = draw_stale_kv(jax.random.fold_in(jax.random.fold_in(splits[10], part), 71), part)
    mask_blocks = draw_mask_blocks(jax.random.fold_in(jax.random.fold_in(splits[10], part), 71), part)
    counts = draw_counts(jax.random.fold_in(jax.random.fold_in(splits[10], part), 71), part)
    return dict(hidden_in=hidden_in, text_rows=text_rows, mod_table=mod_table, timestep=timestep, w_query=w_query, w_out=w_out, w_text=w_text, stale_kv=stale_kv, mask_blocks=mask_blocks, counts=counts)


EPSILON = 1e-06

def layer_norm(values):
    values = values.astype(jnp.float32)
    center = values - lax.optimization_barrier(jnp.mean(values, axis=-1, keepdims=True))
    spread = lax.optimization_barrier(jnp.mean(center * center, axis=-1, keepdims=True))
    return center * lax.rsqrt(spread + EPSILON)

def attend(block_query, image_pairs, text_pairs, live_count):
    joined = jnp.concatenate([text_pairs, image_pairs], axis=0)
    slot = jnp.arange(WIN * BLK, dtype=jnp.int32) // BLK
    live = jnp.concatenate([jnp.ones((TXT,), dtype=jnp.bool_), slot < live_count])
    keys = joined[:, :INNER].astype(jnp.float32).reshape(-1, HEADS, HD)
    values = joined[:, INNER:].astype(jnp.float32).reshape(-1, HEADS, HD)
    query_heads = block_query.astype(jnp.float32).reshape(BLK, HEADS, HD)
    scores = jnp.einsum('qhd,khd->hqk', query_heads, keys) * HD ** (-0.5)
    scores = jnp.where(live[None, None, :], scores, -1e+30)
    peak = lax.optimization_barrier(jnp.max(scores, axis=-1, keepdims=True))
    raised = jnp.exp(scores - peak)
    probs = (raised / lax.optimization_barrier(jnp.sum(raised, axis=-1, keepdims=True))).astype(jnp.bfloat16)
    mixed = jnp.einsum('hqk,khd->qhd', probs.astype(jnp.float32), values)
    return mixed.reshape(BLK, INNER).astype(jnp.bfloat16)

def reference(hidden_in, text_rows, mod_table, timestep, w_query, w_out, w_text, stale_kv, mask_blocks, counts):
    modulations = lax.dynamic_index_in_dim(mod_table, timestep[0], 0, keepdims=False)
    state = hidden_in
    results = []
    for layer in range(LAYERS):
        modulation = modulations[layer]
        conditioned = (text_rows.astype(jnp.float32) * (1.0 + modulation[4]) + modulation[3]).astype(jnp.bfloat16)
        text_pairs = jnp.dot(conditioned, w_text[layer], preferred_element_type=jnp.float32).astype(jnp.bfloat16)
        normed = (layer_norm(state) * (1.0 + modulation[1]) + modulation[0]).astype(jnp.bfloat16)
        query = jnp.dot(normed, w_query[layer], preferred_element_type=jnp.float32).astype(jnp.bfloat16)
        stale_blocks = stale_kv[layer].reshape(NBLK, BLK, 2 * INNER)

        def per_block(items):
            block_query, chosen, live_count = items
            image_pairs = jnp.take(stale_blocks, chosen, axis=0).reshape(WIN * BLK, 2 * INNER)
            return attend(block_query, image_pairs, text_pairs, live_count)
        attended = lax.map(per_block, (query.reshape(NBLK, BLK, INNER), mask_blocks, counts))
        attended = attended.reshape(SEQ, INNER)
        projected = jnp.dot(attended, w_out[layer], preferred_element_type=jnp.float32)
        state = (state.astype(jnp.float32) + modulation[2] * projected).astype(jnp.bfloat16)
        results.append(state)
    return jnp.stack(results, axis=0)
```

```python
import functools

import jax
import jax.numpy as jnp
from jax import lax
from jax.experimental import pallas as pl
from jax.experimental.pallas import tpu as pltpu
from jax.sharding import PartitionSpec as P

HD = 128
BLK = 128
EPSILON = 1e-06
MESH = pl.DeviceIdType.MESH
ROWS = 16


def exclusive_rows(rows):
    return max(rows * 5 // 12 // ROWS, 1) * ROWS


def gather_kernel(
    n, wq, wo, kv, part, wq_all, wo_all, kv_rim, text,
    sums, total, ring_send, ring_recv, mate_send, mate_recv,
    rim_send, rim_recv, text_send, text_recv, share_send, share_recv, local_sem,
):
    me = lax.axis_index("patch")
    group = lax.axis_index("groups")
    parity = lax.rem(group, 2)
    mate = group + 1 - 2 * parity
    half = n // 2
    odd = lax.rem(me, 2)
    place = (1 - odd) * lax.div(me, 2) + odd * (n - 1 - lax.div(me, 2))

    def at(position):
        position = lax.rem(position + n, n)
        high = lax.div(position, half)
        return (1 - high) * 2 * position + high * (2 * (n - 1 - position) + 1)

    right, left = at(place + 1), at(place - 1)
    peers = [lax.rem(me + step, n) for step in range(1, n)]

    barrier = pltpu.get_barrier_semaphore()
    for peer in peers:
        pl.semaphore_signal(barrier, inc=1, device_id={"patch": peer}, device_id_type=MESH)
    pl.semaphore_signal(barrier, inc=1, device_id={"groups": mate}, device_id_type=MESH)
    pl.semaphore_wait(barrier, n)

    flows = (
        (wq, wq_all, -1, half),
        (wq, wq_all, 1, half - 1),
        (wo, wo_all, -1, half - 1),
        (wo, wo_all, 1, half),
    )

    def remote(src, dst, send, recv, target):
        return pltpu.make_async_remote_copy(
            src_ref=src, dst_ref=dst, send_sem=send, recv_sem=recv,
            device_id=target, device_id_type=MESH,
        )

    def rows_of(own):
        rows = own.shape[0]
        apart = exclusive_rows(rows)
        return rows, apart, rows - apart

    def span(start, size):
        return pl.ds(pl.multiple_of(start, ROWS), size)

    def ring(flow, hop, received=False):
        own, every, way, _ = flows[flow]
        _, apart, keep = rows_of(own)
        shard = at(place + way * (hop if received else hop - 1))
        window = span(parity * apart, keep)
        dst = every.at[shard, window]
        src = own.at[window] if hop == 1 and not received else dst
        target = {"patch": right if way < 0 else left}
        return remote(src, dst, ring_send.at[flow, hop - 1], ring_recv.at[flow, hop - 1], target)

    def across(flow, hop, received=False):
        own, every, way, _ = flows[flow]
        _, apart, keep = rows_of(own)
        shard = at(place + way * hop)
        side = 1 - parity if received else parity
        ref = every.at[shard, span(side * keep, apart)]
        return remote(ref, ref, mate_send.at[flow, hop - 1], mate_recv.at[flow, hop - 1], {"groups": mate})

    blocks = kv.shape[0] // BLK

    def rim(side, block, received=False):
        window = pl.ds(block * BLK, BLK)
        slot = side if not received else side
        target = {"patch": me + 1 if side == 0 else me - 1}
        return remote(
            kv.at[window], kv_rim.at[slot, window],
            rim_send.at[side, block], rim_recv.at[side, block], target,
        )

    def rim_start(block):
        @pl.when(me < n - 1)
        def _():
            rim(0, block).start()

        @pl.when(me > 0)
        def _():
            rim(1, block).start()

    def scatter(step, received=False):
        peer = lax.rem(me + step, n)
        source = lax.rem(me + n - step, n)
        return remote(
            part.at[peer], sums.at[source if received else me],
            text_send.at[step - 1], text_recv.at[step - 1], {"patch": peer},
        )

    def share(step, received=False):
        peer = lax.rem(me + step, n)
        source = lax.rem(me + n - step, n)
        slot = source if received else me
        return remote(
            text.at[slot], text.at[slot],
            share_send.at[step - 1], share_recv.at[step - 1], {"patch": peer},
        )

    for flow in range(4):
        ring(flow, 1).start()
    own_sum = pltpu.make_async_copy(part.at[me], sums.at[me], local_sem.at[0])
    own_sum.start()
    for step in range(1, n):
        scatter(step).start()

    started = 0
    for hop in range(1, half + 1):
        if started < blocks:
            rim_start(started)
            started += 1
        for flow in range(4):
            if hop <= flows[flow][3]:
                ring(flow, hop, True).wait_recv()
                if hop < flows[flow][3]:
                    ring(flow, hop + 1).start()
                across(flow, hop).start()
        if hop == 1:
            own_sum.wait()
            for step in range(1, n):
                scatter(step, True).wait_recv()
            total[...] = jnp.sum(sums[...], axis=0).astype(total.dtype)
            keep_sum = pltpu.make_async_copy(total, text.at[me], local_sem.at[1])
            keep_sum.start()
            keep_sum.wait()
            for step in range(1, n):
                share(step).start()
    for block in range(started, blocks):
        rim_start(block)

    for flow in range(4):
        for hop in range(1, flows[flow][3] + 1):
            across(flow, hop, True).wait_recv()
            across(flow, hop).wait_send()
            ring(flow, hop).wait_send()
    for step in range(1, n):
        scatter(step).wait_send()
        share(step).wait_send()
        share(step, True).wait_recv()
    for block in range(blocks):
        @pl.when(me < n - 1)
        def _():
            rim(0, block).wait_send()
            rim(1, block).wait_recv()

        @pl.when(me > 0)
        def _():
            rim(1, block).wait_send()
            rim(0, block).wait_recv()


def gather_all(n, wq, wo, kv, part):
    half = n // 2
    blocks = kv.shape[0] // BLK
    anywhere = pl.BlockSpec(memory_space=pl.ANY)
    dma = pltpu.SemaphoreType.DMA
    return pl.pallas_call(
        functools.partial(gather_kernel, n),
        out_shape=(
            jax.ShapeDtypeStruct((n,) + wq.shape, wq.dtype),
            jax.ShapeDtypeStruct((n,) + wo.shape, wo.dtype),
            jax.ShapeDtypeStruct((2,) + kv.shape, kv.dtype),
            jax.ShapeDtypeStruct(part.shape, jnp.bfloat16),
        ),
        in_specs=[anywhere] * 4,
        out_specs=(anywhere,) * 4,
        scratch_shapes=[
            pltpu.VMEM(part.shape, jnp.float32),
            pltpu.VMEM(part.shape[1:], jnp.bfloat16),
            dma((4, half)), dma((4, half)), dma((4, half)), dma((4, half)),
            dma((2, blocks)), dma((2, blocks)),
            dma((n - 1,)), dma((n - 1,)), dma((n - 1,)), dma((n - 1,)),
            dma((2,)),
        ],
        compiler_params=pltpu.CompilerParams(collective_id=0, has_side_effects=True),
        name="gather_all",
    )(wq, wo, kv, part)


def layer_kernel(
    scalars, chosen, counts, state, modulation, wq, wo, wq_all, wo_all, kv, kv_rim, text, out,
    wq_full, wo_full, joined, normed, query, mixed, wq_sem, wo_sem, kv_sem, text_sem,
):
    n = wq_all.shape[0]
    me = scalars[0]
    tokens, width = state.shape
    blocks = tokens // BLK
    inner = query.shape[1]
    heads = inner // HD
    spread = chosen.shape[1]
    keys = joined.shape[1]
    lead = keys - spread * BLK

    def fetch(own, every, full, sem):
        rows = own.shape[0]
        for shard in range(n):
            target = full.at[pl.ds(shard * rows, rows)]

            @pl.when(me == shard)
            def _():
                pltpu.make_async_copy(own, target, sem.at[shard]).start()

            @pl.when(me != shard)
            def _():
                pltpu.make_async_copy(every.at[shard], target, sem.at[shard]).start()

    def fetched(own, full, sem):
        rows = own.shape[0]
        for shard in range(n):
            pltpu.make_async_copy(own, full.at[pl.ds(shard * rows, rows)], sem.at[shard]).wait()

    fetch(wq, wq_all, wq_full, wq_sem)
    for block in range(blocks):
        pltpu.make_async_copy(text, joined.at[block, pl.ds(0, lead)], text_sem.at[block]).start()
        for slot in range(spread):
            pick = chosen[block, slot] - (me - 1) * blocks
            home = lax.div(pick, blocks)
            row = pl.multiple_of(lax.rem(pick, blocks) * BLK, BLK)
            target = joined.at[block, pl.ds(lead + slot * BLK, BLK)]

            @pl.when(home == 1)
            def _():
                pltpu.make_async_copy(kv.at[pl.ds(row, BLK)], target, kv_sem.at[block, slot]).start()

            @pl.when(home != 1)
            def _():
                pltpu.make_async_copy(
                    kv_rim.at[lax.div(home, 2), pl.ds(row, BLK)], target, kv_sem.at[block, slot]
                ).start()
    fetch(wo, wo_all, wo_full, wo_sem)

    step = 16

    @pl.loop(0, tokens // step)
    def _(index):
        window = pl.ds(pl.multiple_of(index * step, step), step)
        values = state[window, :].astype(jnp.float32)
        center = values - jnp.mean(values, axis=-1, keepdims=True)
        variance = jnp.mean(center * center, axis=-1, keepdims=True)
        scaled = center * lax.rsqrt(variance + EPSILON)
        normed[window, :] = (
            scaled * (1.0 + modulation[1:2, :]) + modulation[0:1, :]
        ).astype(normed.dtype)

    fetched(wq, wq_full, wq_sem)
    tile = 256

    @pl.loop(0, inner // tile)
    def _(index):
        window = pl.ds(pl.multiple_of(index * tile, tile), tile)
        query[:, window] = jnp.dot(
            normed[...], wq_full[:, window], preferred_element_type=jnp.float32
        ).astype(query.dtype)

    for block in range(blocks):
        pltpu.make_async_copy(text, joined.at[block, pl.ds(0, lead)], text_sem.at[block]).wait()
        for slot in range(spread):
            target = joined.at[block, pl.ds(lead + slot * BLK, BLK)]
            pltpu.make_async_copy(kv.at[pl.ds(0, BLK)], target, kv_sem.at[block, slot]).wait()

    together = 4 if heads % 4 == 0 else 1
    bunches = heads // together

    @pl.loop(0, blocks * bunches)
    def _(index):
        block = lax.div(index, bunches)
        bunch = lax.rem(index, bunches)
        rows = pl.ds(pl.multiple_of(block * BLK, BLK), BLK)
        limit = lead + counts[block] * BLK
        live = lax.broadcasted_iota(jnp.int32, (BLK, keys), 1) < limit
        for one in range(together):
            start = bunch * (together * HD) + one * HD
            columns = pl.ds(pl.multiple_of(start, HD), HD)
            beyond = pl.ds(pl.multiple_of(inner + start, HD), HD)
            scores = lax.dot_general(
                query[rows, columns], joined[block, :, columns], (((1,), (1,)), ((), ())),
                preferred_element_type=jnp.float32,
            )
            scores = jnp.where(live, scores, -1e30)
            peak = jnp.max(scores, axis=-1, keepdims=True)
            raised = jnp.exp((scores - peak) * HD ** (-0.5))
            whole = jnp.sum(raised, axis=-1, keepdims=True)
            share = jnp.dot(
                raised.astype(jnp.bfloat16), joined[block, :, beyond],
                preferred_element_type=jnp.float32,
            )
            mixed[rows, columns] = (share / whole).astype(mixed.dtype)

    fetched(wo, wo_full, wo_sem)

    @pl.loop(0, width // tile)
    def _(index):
        window = pl.ds(pl.multiple_of(index * tile, tile), tile)
        projected = jnp.dot(mixed[...], wo_full[:, window], preferred_element_type=jnp.float32)
        out[:, window] = (
            state[:, window].astype(jnp.float32) + modulation[2:3, window] * projected
        ).astype(out.dtype)


def layer(scalars, chosen, counts, state, modulation, wq, wo, wq_all, wo_all, kv, kv_rim, text):
    n = wq_all.shape[0]
    tokens, width = state.shape
    blocks = tokens // BLK
    inner = wq.shape[1]
    spread = chosen.shape[1]
    smem = pl.BlockSpec(memory_space=pltpu.SMEM)
    vmem = pl.BlockSpec(memory_space=pltpu.VMEM)
    anywhere = pl.BlockSpec(memory_space=pl.ANY)
    dma = pltpu.SemaphoreType.DMA
    return pl.pallas_call(
        layer_kernel,
        out_shape=jax.ShapeDtypeStruct(state.shape, state.dtype),
        in_specs=[smem] * 3 + [vmem] * 2 + [anywhere] * 7,
        out_specs=vmem,
        scratch_shapes=[
            pltpu.VMEM((n * wq.shape[0], inner), wq.dtype),
            pltpu.VMEM((n * wo.shape[0], width), wo.dtype),
            pltpu.VMEM((blocks, text.shape[0] + spread * BLK, kv.shape[1]), kv.dtype),
            pltpu.VMEM(state.shape, jnp.bfloat16),
            pltpu.VMEM((tokens, inner), jnp.bfloat16),
            pltpu.VMEM((tokens, inner), jnp.bfloat16),
            dma((n,)), dma((n,)), dma((blocks, spread)), dma((blocks,)),
        ],
        compiler_params=pltpu.CompilerParams(vmem_limit_bytes=60 * 2**20),
        name="layer",
    )(scalars, chosen, counts, state, modulation, wq, wo, wq_all, wo_all, kv, kv_rim, text)


def local(
    hidden_in, text_rows, mod_table, timestep, w_query, w_out, w_text, stale_kv, mask_blocks, counts
):
    patch_id = lax.axis_index("patch")
    section_id = lax.axis_index("section")
    n = lax.axis_size("patch")
    width = text_rows.shape[1]
    modulation = lax.dynamic_index_in_dim(mod_table, timestep[0], 0, keepdims=False)[0]
    text_shift = lax.dynamic_slice_in_dim(modulation[3], patch_id * width, width, 0)
    text_scale = lax.dynamic_slice_in_dim(modulation[4], patch_id * width, width, 0)
    conditioned = (text_rows.astype(jnp.float32) * (1.0 + text_scale) + text_shift).astype(
        jnp.bfloat16
    )
    partial_pairs = jnp.dot(conditioned, w_text[0], preferred_element_type=jnp.float32)
    wq, wo, kv = w_query[0], w_out[0], stale_kv[0]
    wq_all, wo_all, kv_rim, text = gather_all(
        n, wq, wo, kv, partial_pairs.reshape(n, ROWS, -1)
    )
    text = text.reshape(partial_pairs.shape)
    scalars = patch_id.astype(jnp.int32).reshape(1)

    def run(state):
        return layer(
            scalars, mask_blocks, counts, state, modulation,
            wq, wo, wq_all, wo_all, kv, kv_rim, text,
        )

    first = run(hidden_in)
    inbox = lax.ppermute(first, "section", [(i, i + 1) for i in range(lax.axis_size("section") - 1)])
    result = run(jnp.where(section_id == 0, hidden_in, inbox))
    return result[None]


def solution(mesh):
    in_specs = (
        P(("groups", "patch"), None),
        P("groups", "patch"),
        P(None, "section", None, None),
        P("groups"),
        P("section", "patch", None),
        P("section", "patch", None),
        P("section", "patch", None),
        P("section", ("groups", "patch"), None),
        P(("groups", "patch"), None),
        P(("groups", "patch")),
    )
    out_specs = P("section", ("groups", "patch"), None)
    return jax.shard_map(local, mesh=mesh, in_specs=in_specs, out_specs=out_specs, check_vma=False)
```

```python
import functools

import jax
import jax.numpy as jnp
from jax import lax
from jax.experimental import pallas as pl
from jax.experimental.pallas import tpu as pltpu
from jax.sharding import PartitionSpec as P

HD = 128
BLK = 128
EPSILON = 1e-06
MESH = pl.DeviceIdType.MESH
ROWS = 16


def exclusive_rows(rows):
    return max(rows * 5 // 12 // ROWS, 1) * ROWS


LAG = 2
TILE = 256


def kernel(
    n, chosen, counts, modulation, state, wq, wo, kv, part, out,
    wq_all, wo_all, kvs, text, sums, total, normed, query, mixed, inbox,
    ring_send, ring_recv, mate_send, mate_recv, rim_send, rim_recv,
    text_send, text_recv, share_send, share_recv, hand_send, hand_recv, own_sem, text_sem,
):
    me = lax.axis_index("patch")
    group = lax.axis_index("groups")
    section = lax.axis_index("section")
    parity = lax.rem(group, 2)
    mate = group + 1 - 2 * parity
    half = n // 2
    odd = lax.rem(me, 2)
    place = (1 - odd) * lax.div(me, 2) + odd * (n - 1 - lax.div(me, 2))
    tokens, width = state.shape
    inner = query.shape[1]
    heads = inner // HD
    blocks = kv.shape[0]
    chunks = part.shape[0]
    spread = chosen.shape[1]
    lead = text.shape[0]
    keys = lead + spread * BLK

    def at(position):
        position = lax.rem(position + n, n)
        high = lax.div(position, half)
        return (1 - high) * 2 * position + high * (2 * (n - 1 - position) + 1)

    def when(needed, condition, action):
        if needed:
            pl.when(condition)(action)
        else:
            action()

    right, left = at(place + 1), at(place - 1)

    own_copies = [
        pltpu.make_async_copy(wq, wq_all.at[pl.ds(pl.multiple_of(me * wq.shape[0], ROWS), wq.shape[0])], own_sem.at[0]),
        pltpu.make_async_copy(wo, wo_all.at[pl.ds(pl.multiple_of(me * wo.shape[0], ROWS), wo.shape[0])], own_sem.at[1]),
        pltpu.make_async_copy(kv, kvs.at[pl.ds(blocks, blocks)], own_sem.at[2]),
    ]

    barrier = pltpu.get_barrier_semaphore()
    for step in range(1, n):
        pl.semaphore_signal(barrier, inc=1, device_id={"patch": lax.rem(me + step, n)}, device_id_type=MESH)
    pl.semaphore_signal(barrier, inc=1, device_id={"groups": mate}, device_id_type=MESH)
    pl.semaphore_signal(barrier, inc=1, device_id={"section": 1 - section}, device_id_type=MESH)
    pl.semaphore_wait(barrier, n + 1)

    flows = (
        (wq, wq_all, -1, half),
        (wq, wq_all, 1, half - 1),
        (wo, wo_all, -1, half - 1),
        (wo, wo_all, 1, half),
    )

    def remote(src, dst, send, recv, target):
        return pltpu.make_async_remote_copy(
            src_ref=src, dst_ref=dst, send_sem=send, recv_sem=recv,
            device_id=target, device_id_type=MESH,
        )

    def span(start, size):
        return pl.ds(pl.multiple_of(start, ROWS), size)

    def ring(flow, hop, received=False):
        own, every, way, _ = flows[flow]
        rows = own.shape[0]
        apart = exclusive_rows(rows)
        keep = rows - apart
        shard = at(place + way * (hop if received else hop - 1))
        dst = every.at[span(shard * rows + parity * apart, keep)]
        src = own.at[span(parity * apart, keep)] if hop == 1 and not received else dst
        target = {"patch": right if way < 0 else left}
        return remote(src, dst, ring_send.at[flow, hop - 1], ring_recv.at[flow, hop - 1], target)

    def across(flow, hop, received=False):
        own, every, way, _ = flows[flow]
        rows = own.shape[0]
        apart = exclusive_rows(rows)
        keep = rows - apart
        shard = at(place + way * hop)
        side = 1 - parity if received else parity
        ref = every.at[span(shard * rows + side * keep, apart)]
        return remote(ref, ref, mate_send.at[flow, hop - 1], mate_recv.at[flow, hop - 1], {"groups": mate})

    def rim(side, block):
        return remote(
            kv.at[block], kvs.at[2 * side * blocks + block],
            rim_send.at[side, block], rim_recv.at[side, block],
            {"patch": me + 1 if side == 0 else me - 1},
        )

    def rim_start(block):
        pl.when(me < n - 1)(lambda: rim(0, block).start())
        pl.when(me > 0)(lambda: rim(1, block).start())

    few = chunks < n

    def scatter(step, received=False):
        peer = lax.rem(me + step, n)
        source = lax.rem(me + n - step, n)
        return remote(
            part.at[jnp.minimum(peer, chunks - 1) if few else peer], sums.at[source if received else me],
            text_send.at[step - 1], text_recv.at[step - 1], {"patch": peer},
        )

    def share(step, received=False):
        peer = lax.rem(me + step, n)
        slot = lax.rem(me + n - step, n) if received else me
        ref = text.at[span((jnp.minimum(slot, chunks - 1) if few else slot) * ROWS, ROWS)]
        return remote(ref, ref, share_send.at[step - 1], share_recv.at[step - 1], {"patch": peer})

    own_chunk = jnp.minimum(me, chunks - 1) if few else me
    own_sum = pltpu.make_async_copy(part.at[own_chunk], sums.at[me], text_sem.at[0])
    keep_sum = pltpu.make_async_copy(total, text.at[span(own_chunk * ROWS, ROWS)], text_sem.at[1])

    def text_start():
        when(few, me < chunks, own_sum.start)
        for step in range(1, n):
            when(few, lax.rem(me + step, n) < chunks, scatter(step).start)

    def text_reduce():
        def reduce():
            own_sum.wait()
            for step in range(1, n):
                scatter(step, True).wait_recv()
            total[...] = jnp.sum(sums[...], axis=0).astype(total.dtype)
            keep_sum.start()
            keep_sum.wait()
            for step in range(1, n):
                share(step).start()

        when(few, me < chunks, reduce)

    def text_arrive():
        for step in range(1, n):
            when(few, lax.rem(me + n - step, n) < chunks, share(step, True).wait_recv)

    def norm(source):
        step = ROWS

        @pl.loop(0, tokens // step)
        def _(index):
            window = pl.ds(pl.multiple_of(index * step, step), step)
            values = source[window, :].astype(jnp.float32)
            center = values - jnp.mean(values, axis=-1, keepdims=True)
            variance = jnp.mean(center * center, axis=-1, keepdims=True)
            scaled = center * lax.rsqrt(variance + EPSILON)
            normed[window, :] = (
                scaled * (1.0 + modulation[1:2, :]) + modulation[0:1, :]
            ).astype(normed.dtype)

    def project_query():
        @pl.loop(0, inner // TILE)
        def _(index):
            window = pl.ds(pl.multiple_of(index * TILE, TILE), TILE)
            query[:, window] = jnp.dot(
                normed[...], wq_all[:, window], preferred_element_type=jnp.float32
            ).astype(query.dtype)

    together = 4 if heads % 4 == 0 else 1

    def attend(first, last):
        bunches = heads // together

        @pl.loop(first * bunches, last * bunches)
        def _(index):
            block = lax.div(index, bunches)
            bunch = lax.rem(index, bunches)
            rows = pl.ds(pl.multiple_of(block * BLK, BLK), BLK)
            limit = lead + counts[block] * BLK
            live = lax.broadcasted_iota(jnp.int32, (BLK, keys), 1) < limit
            picks = [
                jnp.clip(chosen[block, slot] - (me - 1) * blocks, 0, 3 * blocks - 1)
                for slot in range(spread)
            ]
            for one in range(together):
                start = bunch * (together * HD) + one * HD
                columns = pl.ds(pl.multiple_of(start, HD), HD)
                beyond = pl.ds(pl.multiple_of(inner + start, HD), HD)
                key = jnp.concatenate([text[:, columns]] + [kvs[pick, :, columns] for pick in picks], axis=0)
                value = jnp.concatenate([text[:, beyond]] + [kvs[pick, :, beyond] for pick in picks], axis=0)
                scores = lax.dot_general(
                    query[rows, columns], key, (((1,), (1,)), ((), ())),
                    preferred_element_type=jnp.float32,
                )
                scores = jnp.where(live, scores, -1e30)
                peak = jnp.max(scores, axis=-1, keepdims=True)
                raised = jnp.exp((scores - peak) * HD ** (-0.5))
                whole = jnp.sum(raised, axis=-1, keepdims=True)
                share_of = jnp.dot(
                    raised.astype(jnp.bfloat16), value, preferred_element_type=jnp.float32
                )
                mixed[rows, columns] = (share_of / whole).astype(mixed.dtype)

    parts = width // (3 * TILE) if width % (3 * TILE) == 0 else 1
    part_width = width // parts

    def project_out(source, index_from, index_to):
        @pl.loop(index_from, index_to)
        def _(index):
            window = pl.ds(pl.multiple_of(index * TILE, TILE), TILE)
            projected = jnp.dot(mixed[...], wo_all[:, window], preferred_element_type=jnp.float32)
            out[:, window] = (
                source[:, window].astype(jnp.float32) + modulation[2:3, window] * projected
            ).astype(out.dtype)

    def hand(index):
        window = pl.ds(index * part_width, part_width)
        return remote(
            out.at[:, window], inbox.at[:, window],
            hand_send.at[index], hand_recv.at[index], {"section": 1 - section},
        )

    def relay(flow, hop):
        if hop <= flows[flow][3]:
            ring(flow, hop, True).wait_recv()
            if hop < flows[flow][3]:
                ring(flow, hop + 1).start()
            across(flow, hop).start()

    ring(0, 1).start()
    ring(1, 1).start()
    text_start()
    for copy in own_copies:
        copy.start()
    rim_start(0)
    started = 1
    pl.when(section == 0)(lambda: norm(state))
    for hop in range(1, half + 1):
        relay(0, hop)
        relay(1, hop)
        if hop == max(LAG - 1, 1):
            ring(2, 1).start()
            ring(3, 1).start()
        if hop > LAG:
            relay(2, hop - LAG)
            relay(3, hop - LAG)
        if hop == 1:
            text_reduce()
        if started < blocks:
            rim_start(started)
            started += 1
    for block in range(started, blocks):
        rim_start(block)

    def wait_query():
        for flow in range(2):
            for hop in range(1, flows[flow][3] + 1):
                across(flow, hop, True).wait_recv()
        own_copies[0].wait()

    def wait_keys():
        own_copies[2].wait()
        for block in range(blocks):
            pl.when(me < n - 1)(lambda: rim(1, block).wait_recv())
            pl.when(me > 0)(lambda: rim(0, block).wait_recv())
        text_arrive()

    todo = [h for h in range(half - LAG + 1, half + 1)]

    def relay_next():
        if todo:
            hop = todo.pop(0)
            relay(2, hop)
            relay(3, hop)

    wait_query()
    pl.when(section == 0)(project_query)
    relay_next()
    wait_keys()
    for block in range(blocks):
        pl.when(section == 0)(lambda: attend(block, block + 1))
        relay_next()
    while todo:
        relay_next()
    for flow in range(2, 4):
        for hop in range(1, flows[flow][3] + 1):
            across(flow, hop, True).wait_recv()
    own_copies[1].wait()

    each = part_width // TILE

    @pl.when(section == 0)
    def _():
        for index in range(parts):
            project_out(state, index * each, (index + 1) * each)
            if index:
                hand(index - 1).start()
        hand(parts - 1).start()

    @pl.when(section == 1)
    def _():
        for index in range(parts):
            hand(index).wait_recv()
        norm(inbox)
        project_query()
        attend(0, blocks)
        project_out(inbox, 0, width // TILE)

    for flow in range(4):
        for hop in range(1, flows[flow][3] + 1):
            across(flow, hop).wait_send()
            ring(flow, hop).wait_send()
    for step in range(1, n):
        when(few, lax.rem(me + step, n) < chunks, scatter(step).wait_send)
        when(few, me < chunks, share(step).wait_send)
    for block in range(blocks):
        pl.when(me < n - 1)(lambda: rim(0, block).wait_send())
        pl.when(me > 0)(lambda: rim(1, block).wait_send())

    @pl.when(section == 0)
    def _():
        for index in range(parts):
            hand(index).wait_send()


def run(n, chosen, counts, modulation, state, wq, wo, kv, part):
    half = n // 2
    tokens, width = state.shape
    inner = wq.shape[1]
    blocks = kv.shape[0]
    smem = pl.BlockSpec(memory_space=pltpu.SMEM)
    vmem = pl.BlockSpec(memory_space=pltpu.VMEM)
    anywhere = pl.BlockSpec(memory_space=pl.ANY)
    dma = pltpu.SemaphoreType.DMA
    parts = width // (3 * TILE) if width % (3 * TILE) == 0 else 1
    b16 = jnp.bfloat16
    return pl.pallas_call(
        functools.partial(kernel, n),
        out_shape=jax.ShapeDtypeStruct(state.shape, state.dtype),
        in_specs=[smem, smem, vmem, vmem] + [anywhere] * 4,
        out_specs=vmem,
        scratch_shapes=[
            pltpu.VMEM((n * wq.shape[0], inner), b16),
            pltpu.VMEM((n * wo.shape[0], width), b16),
            pltpu.VMEM((3 * blocks,) + kv.shape[1:], b16),
            pltpu.VMEM((part.shape[0] * ROWS, kv.shape[2]), b16),
            pltpu.VMEM((n,) + part.shape[1:], jnp.float32),
            pltpu.VMEM(part.shape[1:], b16),
            pltpu.VMEM((tokens, width), b16),
            pltpu.VMEM((tokens, inner), b16),
            pltpu.VMEM((tokens, inner), b16),
            pltpu.VMEM((tokens, width), b16),
            dma((4, half)), dma((4, half)), dma((4, half)), dma((4, half)),
            dma((2, blocks)), dma((2, blocks)),
            dma((n - 1,)), dma((n - 1,)), dma((n - 1,)), dma((n - 1,)),
            dma((parts,)), dma((parts,)), dma((3,)), dma((2,)),
        ],
        compiler_params=pltpu.CompilerParams(
            collective_id=0, has_side_effects=True, vmem_limit_bytes=60 * 2**20
        ),
        name="layers",
    )(chosen, counts, modulation, state, wq, wo, kv, part)


def local(
    hidden_in, text_rows, mod_table, timestep, w_query, w_out, w_text, stale_kv, mask_blocks, counts
):
    patch_id = lax.axis_index("patch")
    n = lax.axis_size("patch")
    width = text_rows.shape[1]
    modulation = lax.dynamic_index_in_dim(mod_table, timestep[0], 0, keepdims=False)[0]
    text_shift = lax.dynamic_slice_in_dim(modulation[3], patch_id * width, width, 0)
    text_scale = lax.dynamic_slice_in_dim(modulation[4], patch_id * width, width, 0)
    conditioned = (text_rows.astype(jnp.float32) * (1.0 + text_scale) + text_shift).astype(
        jnp.bfloat16
    )
    partial_pairs = jnp.dot(conditioned, w_text[0], preferred_element_type=jnp.float32)
    kv = stale_kv[0].reshape(-1, BLK, stale_kv.shape[2])
    part = partial_pairs.reshape(-1, ROWS, partial_pairs.shape[1])
    result = run(n, mask_blocks, counts, modulation, hidden_in, w_query[0], w_out[0], kv, part)
    return result[None]


def solution(mesh):
    in_specs = (
        P(("groups", "patch"), None),
        P("groups", "patch"),
        P(None, "section", None, None),
        P("groups"),
        P("section", "patch", None),
        P("section", "patch", None),
        P("section", "patch", None),
        P("section", ("groups", "patch"), None),
        P(("groups", "patch"), None),
        P(("groups", "patch")),
    )
    out_specs = P("section", ("groups", "patch"), None)
    return jax.shard_map(local, mesh=mesh, in_specs=in_specs, out_specs=out_specs, check_vma=False)
```

```python
import functools

import jax
import jax.numpy as jnp
from jax import lax
from jax.experimental import pallas as pl
from jax.experimental.pallas import tpu as pltpu
from jax.sharding import PartitionSpec as P

HD = 128
BLK = 128
EPSILON = 1e-06
MESH = pl.DeviceIdType.MESH
ROWS = 16


def exclusive_rows(rows):
    return max(rows * 5 // 12 // ROWS, 1) * ROWS


LAG = 0
TILE = 256


def kernel(
    n, chosen, counts, modulation, state, wq, wo, kv, part, out,
    wq_all, wo_all, kvs, text, sums, total, normed, query, mixed, inbox,
    ring_send, ring_recv, mate_send, mate_recv, rim_send, rim_recv,
    text_send, text_recv, share_send, share_recv, hand_send, hand_recv, own_sem, text_sem,
):
    me = lax.axis_index("patch")
    group = lax.axis_index("groups")
    section = lax.axis_index("section")
    parity = lax.rem(group, 2)
    mate = group + 1 - 2 * parity
    half = n // 2
    odd = lax.rem(me, 2)
    place = (1 - odd) * lax.div(me, 2) + odd * (n - 1 - lax.div(me, 2))
    tokens, width = state.shape
    inner = query.shape[1]
    heads = inner // HD
    blocks = kv.shape[0]
    chunks = part.shape[0]
    spread = chosen.shape[1]
    lead = text.shape[0]
    keys = lead + spread * BLK

    def at(position):
        position = lax.rem(position + n, n)
        high = lax.div(position, half)
        return (1 - high) * 2 * position + high * (2 * (n - 1 - position) + 1)

    def when(needed, condition, action):
        if needed:
            pl.when(condition)(action)
        else:
            action()

    right, left = at(place + 1), at(place - 1)

    own_copies = [
        pltpu.make_async_copy(wq, wq_all.at[pl.ds(pl.multiple_of(me * wq.shape[0], ROWS), wq.shape[0])], own_sem.at[0]),
        pltpu.make_async_copy(wo, wo_all.at[pl.ds(pl.multiple_of(me * wo.shape[0], ROWS), wo.shape[0])], own_sem.at[1]),
        pltpu.make_async_copy(kv, kvs.at[pl.ds(blocks, blocks)], own_sem.at[2]),
    ]

    barrier = pltpu.get_barrier_semaphore()
    for step in range(1, n):
        pl.semaphore_signal(barrier, inc=1, device_id={"patch": lax.rem(me + step, n)}, device_id_type=MESH)
    pl.semaphore_signal(barrier, inc=1, device_id={"groups": mate}, device_id_type=MESH)
    pl.semaphore_signal(barrier, inc=1, device_id={"section": 1 - section}, device_id_type=MESH)
    pl.semaphore_wait(barrier, n + 1)

    flows = (
        (wq, wq_all, -1, half),
        (wq, wq_all, 1, half - 1),
        (wo, wo_all, -1, half - 1),
        (wo, wo_all, 1, half),
    )

    def remote(src, dst, send, recv, target):
        return pltpu.make_async_remote_copy(
            src_ref=src, dst_ref=dst, send_sem=send, recv_sem=recv,
            device_id=target, device_id_type=MESH,
        )

    def span(start, size):
        return pl.ds(pl.multiple_of(start, ROWS), size)

    def ring(flow, hop, received=False):
        own, every, way, _ = flows[flow]
        rows = own.shape[0]
        apart = exclusive_rows(rows)
        keep = rows - apart
        shard = at(place + way * (hop if received else hop - 1))
        dst = every.at[span(shard * rows + parity * apart, keep)]
        src = own.at[span(parity * apart, keep)] if hop == 1 and not received else dst
        target = {"patch": right if way < 0 else left}
        return remote(src, dst, ring_send.at[flow, hop - 1], ring_recv.at[flow, hop - 1], target)

    def across(flow, hop, received=False):
        own, every, way, _ = flows[flow]
        rows = own.shape[0]
        apart = exclusive_rows(rows)
        keep = rows - apart
        shard = at(place + way * hop)
        side = 1 - parity if received else parity
        ref = every.at[span(shard * rows + side * keep, apart)]
        return remote(ref, ref, mate_send.at[flow, hop - 1], mate_recv.at[flow, hop - 1], {"groups": mate})

    pair = me + 1 - 2 * odd
    onward, behind = me + 2 - 4 * odd, me - 2 + 4 * odd
    has_onward = (onward >= 0) & (onward < n)
    has_behind = (behind >= 0) & (behind < n)

    def rim(leg, block, received=False):
        near, far = 2 * (1 - odd) * blocks + block, 2 * odd * blocks + block
        if received:
            dst = kvs.at[far if leg else near]
        else:
            dst = kvs.at[far]
        src = kvs.at[near] if leg else kv.at[block]
        return remote(
            src, dst, rim_send.at[leg, block], rim_recv.at[leg, block],
            {"patch": onward if leg else pair},
        )

    def rim_forward(block):
        rim(0, block, True).wait_recv()
        pl.when(has_onward)(lambda: rim(1, block).start())

    few = chunks < n

    def scatter(step, received=False):
        peer = lax.rem(me + step, n)
        source = lax.rem(me + n - step, n)
        return remote(
            part.at[jnp.minimum(peer, chunks - 1) if few else peer], sums.at[source if received else me],
            text_send.at[step - 1], text_recv.at[step - 1], {"patch": peer},
        )

    def share(step, received=False):
        peer = lax.rem(me + step, n)
        slot = lax.rem(me + n - step, n) if received else me
        ref = text.at[span((jnp.minimum(slot, chunks - 1) if few else slot) * ROWS, ROWS)]
        return remote(ref, ref, share_send.at[step - 1], share_recv.at[step - 1], {"patch": peer})

    own_chunk = jnp.minimum(me, chunks - 1) if few else me
    own_sum = pltpu.make_async_copy(part.at[own_chunk], sums.at[me], text_sem.at[0])
    keep_sum = pltpu.make_async_copy(total, text.at[span(own_chunk * ROWS, ROWS)], text_sem.at[1])

    def text_start():
        when(few, me < chunks, own_sum.start)
        for step in range(1, n):
            when(few, lax.rem(me + step, n) < chunks, scatter(step).start)

    def text_reduce():
        def reduce():
            own_sum.wait()
            for step in range(1, n):
                scatter(step, True).wait_recv()
            total[...] = jnp.sum(sums[...].astype(jnp.float32), axis=0).astype(total.dtype)
            keep_sum.start()
            keep_sum.wait()
            for step in range(1, n):
                share(step).start()

        when(few, me < chunks, reduce)

    def text_arrive():
        for step in range(1, n):
            when(few, lax.rem(me + n - step, n) < chunks, share(step, True).wait_recv)

    def norm(source):
        step = ROWS

        @pl.loop(0, tokens // step)
        def _(index):
            window = pl.ds(pl.multiple_of(index * step, step), step)
            values = source[window, :].astype(jnp.float32)
            center = values - jnp.mean(values, axis=-1, keepdims=True)
            variance = jnp.mean(center * center, axis=-1, keepdims=True)
            scaled = center * lax.rsqrt(variance + EPSILON)
            normed[window, :] = (
                scaled * (1.0 + modulation[1:2, :]) + modulation[0:1, :]
            ).astype(normed.dtype)

    def project_query():
        @pl.loop(0, inner // TILE)
        def _(index):
            window = pl.ds(pl.multiple_of(index * TILE, TILE), TILE)
            query[:, window] = jnp.dot(
                normed[...], wq_all[:, window], preferred_element_type=jnp.float32
            ).astype(query.dtype)

    together = 4 if heads % 4 == 0 else 1

    def attend(first, last):
        bunches = heads // together

        @pl.loop(first * bunches, last * bunches)
        def _(index):
            block = lax.div(index, bunches)
            bunch = lax.rem(index, bunches)
            rows = pl.ds(pl.multiple_of(block * BLK, BLK), BLK)
            limit = lead + counts[block] * BLK
            live = lax.broadcasted_iota(jnp.int32, (BLK, keys), 1) < limit
            picks = [
                jnp.clip(chosen[block, slot] - (me - 1) * blocks, 0, 3 * blocks - 1)
                for slot in range(spread)
            ]
            for one in range(together):
                start = bunch * (together * HD) + one * HD
                columns = pl.ds(pl.multiple_of(start, HD), HD)
                beyond = pl.ds(pl.multiple_of(inner + start, HD), HD)
                key = jnp.concatenate([text[:, columns]] + [kvs[pick, :, columns] for pick in picks], axis=0)
                value = jnp.concatenate([text[:, beyond]] + [kvs[pick, :, beyond] for pick in picks], axis=0)
                scores = lax.dot_general(
                    query[rows, columns], key, (((1,), (1,)), ((), ())),
                    preferred_element_type=jnp.float32,
                )
                scores = jnp.where(live, scores, -1e30)
                peak = jnp.max(scores, axis=-1, keepdims=True)
                raised = jnp.exp((scores - peak) * HD ** (-0.5))
                whole = jnp.sum(raised, axis=-1, keepdims=True)
                share_of = jnp.dot(
                    raised.astype(jnp.bfloat16), value, preferred_element_type=jnp.float32
                )
                mixed[rows, columns] = (share_of / whole).astype(mixed.dtype)

    parts = width // (3 * TILE) if width % (3 * TILE) == 0 else 1
    part_width = width // parts

    def project_out(source, index_from, index_to):
        @pl.loop(index_from, index_to)
        def _(index):
            window = pl.ds(pl.multiple_of(index * TILE, TILE), TILE)
            projected = jnp.dot(mixed[...], wo_all[:, window], preferred_element_type=jnp.float32)
            out[:, window] = (
                source[:, window].astype(jnp.float32) + modulation[2:3, window] * projected
            ).astype(out.dtype)

    def hand(index):
        window = pl.ds(index * part_width, part_width)
        return remote(
            out.at[:, window], inbox.at[:, window],
            hand_send.at[index], hand_recv.at[index], {"section": 1 - section},
        )

    def relay(flow, hop):
        if hop <= flows[flow][3]:
            ring(flow, hop, True).wait_recv()
            if hop < flows[flow][3]:
                ring(flow, hop + 1).start()
            across(flow, hop).start()

    ring(0, 1).start()
    ring(1, 1).start()
    text_start()
    if LAG < 2:
        ring(2, 1).start()
        ring(3, 1).start()
    for copy in own_copies:
        copy.start()
    for block in range(blocks):
        rim(0, block).start()
    forwarded = 0
    pl.when(section == 0)(lambda: norm(state))
    for hop in range(1, half + 1):
        relay(0, hop)
        relay(1, hop)
        if hop == LAG - 1:
            ring(2, 1).start()
            ring(3, 1).start()
        if hop > LAG:
            relay(2, hop - LAG)
            relay(3, hop - LAG)
        if hop == max(half - 1, 1):
            text_reduce()
        if 2 <= hop and forwarded < blocks:
            rim_forward(forwarded)
            forwarded += 1
    for block in range(forwarded, blocks):
        rim_forward(block)

    def wait_query():
        for flow in range(2):
            for hop in range(1, flows[flow][3] + 1):
                across(flow, hop, True).wait_recv()
        own_copies[0].wait()

    def wait_keys():
        own_copies[2].wait()
        for block in range(blocks):
            pl.when(has_behind)(lambda: rim(1, block, True).wait_recv())
        text_arrive()

    todo = [h for h in range(half - LAG + 1, half + 1)]

    def relay_next():
        if todo:
            hop = todo.pop(0)
            relay(2, hop)
            relay(3, hop)

    wait_query()
    pl.when(section == 0)(project_query)
    relay_next()
    wait_keys()
    for block in range(blocks):
        pl.when(section == 0)(lambda: attend(block, block + 1))
        relay_next()
    while todo:
        relay_next()
    for flow in range(2, 4):
        for hop in range(1, flows[flow][3] + 1):
            across(flow, hop, True).wait_recv()
    own_copies[1].wait()

    each = part_width // TILE

    @pl.when(section == 0)
    def _():
        for index in range(parts):
            project_out(state, index * each, (index + 1) * each)
            if index:
                hand(index - 1).start()
        hand(parts - 1).start()

    @pl.when(section == 1)
    def _():
        for index in range(parts):
            hand(index).wait_recv()
        norm(inbox)
        project_query()
        attend(0, blocks)
        project_out(inbox, 0, width // TILE)

    for flow in range(4):
        for hop in range(1, flows[flow][3] + 1):
            across(flow, hop).wait_send()
            ring(flow, hop).wait_send()
    for step in range(1, n):
        when(few, lax.rem(me + step, n) < chunks, scatter(step).wait_send)
        when(few, me < chunks, share(step).wait_send)
    for block in range(blocks):
        rim(0, block).wait_send()
        pl.when(has_onward)(lambda: rim(1, block).wait_send())

    @pl.when(section == 0)
    def _():
        for index in range(parts):
            hand(index).wait_send()


def run(n, chosen, counts, modulation, state, wq, wo, kv, part):
    half = n // 2
    tokens, width = state.shape
    inner = wq.shape[1]
    blocks = kv.shape[0]
    smem = pl.BlockSpec(memory_space=pltpu.SMEM)
    vmem = pl.BlockSpec(memory_space=pltpu.VMEM)
    anywhere = pl.BlockSpec(memory_space=pl.ANY)
    dma = pltpu.SemaphoreType.DMA
    parts = width // (3 * TILE) if width % (3 * TILE) == 0 else 1
    b16 = jnp.bfloat16
    return pl.pallas_call(
        functools.partial(kernel, n),
        out_shape=jax.ShapeDtypeStruct(state.shape, state.dtype),
        in_specs=[smem, smem, vmem, vmem] + [anywhere] * 4,
        out_specs=vmem,
        scratch_shapes=[
            pltpu.VMEM((n * wq.shape[0], inner), b16),
            pltpu.VMEM((n * wo.shape[0], width), b16),
            pltpu.VMEM((3 * blocks,) + kv.shape[1:], b16),
            pltpu.VMEM((part.shape[0] * ROWS, kv.shape[2]), b16),
            pltpu.VMEM((n,) + part.shape[1:], part.dtype),
            pltpu.VMEM(part.shape[1:], b16),
            pltpu.VMEM((tokens, width), b16),
            pltpu.VMEM((tokens, inner), b16),
            pltpu.VMEM((tokens, inner), b16),
            pltpu.VMEM((tokens, width), b16),
            dma((4, half)), dma((4, half)), dma((4, half)), dma((4, half)),
            dma((2, blocks)), dma((2, blocks)),
            dma((n - 1,)), dma((n - 1,)), dma((n - 1,)), dma((n - 1,)),
            dma((parts,)), dma((parts,)), dma((3,)), dma((2,)),
        ],
        compiler_params=pltpu.CompilerParams(
            collective_id=0, has_side_effects=True, vmem_limit_bytes=60 * 2**20
        ),
        name="layers",
    )(chosen, counts, modulation, state, wq, wo, kv, part)


def local(
    hidden_in, text_rows, mod_table, timestep, w_query, w_out, w_text, stale_kv, mask_blocks, counts
):
    patch_id = lax.axis_index("patch")
    n = lax.axis_size("patch")
    width = text_rows.shape[1]
    modulation = lax.dynamic_index_in_dim(mod_table, timestep[0], 0, keepdims=False)[0]
    text_shift = lax.dynamic_slice_in_dim(modulation[3], patch_id * width, width, 0)
    text_scale = lax.dynamic_slice_in_dim(modulation[4], patch_id * width, width, 0)
    conditioned = (text_rows.astype(jnp.float32) * (1.0 + text_scale) + text_shift).astype(
        jnp.bfloat16
    )
    partial_pairs = jnp.dot(conditioned, w_text[0], preferred_element_type=jnp.float32)
    partial_pairs = partial_pairs.astype(jnp.bfloat16)
    kv = stale_kv[0].reshape(-1, BLK, stale_kv.shape[2])
    part = partial_pairs.reshape(-1, ROWS, partial_pairs.shape[1])
    result = run(n, mask_blocks, counts, modulation, hidden_in, w_query[0], w_out[0], kv, part)
    return result[None]


def solution(mesh):
    in_specs = (
        P(("groups", "patch"), None),
        P("groups", "patch"),
        P(None, "section", None, None),
        P("groups"),
        P("section", "patch", None),
        P("section", "patch", None),
        P("section", "patch", None),
        P("section", ("groups", "patch"), None),
        P(("groups", "patch"), None),
        P(("groups", "patch")),
    )
    out_specs = P("section", ("groups", "patch"), None)
    return jax.shard_map(local, mesh=mesh, in_specs=in_specs, out_specs=out_specs, check_vma=False)
```

```python
import functools

import jax
import jax.numpy as jnp
from jax import lax
from jax.experimental import pallas as pl
from jax.experimental.pallas import tpu as pltpu
from jax.sharding import PartitionSpec as P

HD = 128
BLK = 128
EPSILON = 1e-06
MESH = pl.DeviceIdType.MESH
ROWS = 16


def exclusive_rows(rows):
    return max(rows * 5 // 12 // ROWS, 1) * ROWS


LAG = 0
TILE = 256


def kernel(
    n, chosen, counts, modulation, state, wq, wo, kv, part, out,
    wq_all, wo_all, kvs, text, sums, total, normed, query, mixed, inbox,
    ring_send, ring_recv, mate_send, mate_recv, rim_send, rim_recv,
    text_send, text_recv, share_send, share_recv, hand_send, hand_recv, own_sem, text_sem,
):
    me = lax.axis_index("patch")
    group = lax.axis_index("groups")
    section = lax.axis_index("section")
    parity = lax.rem(group, 2)
    mate = group + 1 - 2 * parity
    half = n // 2
    odd = lax.rem(me, 2)
    place = (1 - odd) * lax.div(me, 2) + odd * (n - 1 - lax.div(me, 2))
    tokens, width = state.shape
    inner = query.shape[1]
    heads = inner // HD
    blocks = kv.shape[0]
    chunks = part.shape[0]
    spread = chosen.shape[1]
    lead = text.shape[0]
    keys = lead + spread * BLK

    def at(position):
        position = lax.rem(position + n, n)
        high = lax.div(position, half)
        return (1 - high) * 2 * position + high * (2 * (n - 1 - position) + 1)

    def when(needed, condition, action):
        if needed:
            pl.when(condition)(action)
        else:
            action()

    right, left = at(place + 1), at(place - 1)

    own_copies = [
        pltpu.make_async_copy(wq, wq_all.at[pl.ds(pl.multiple_of(me * wq.shape[0], ROWS), wq.shape[0])], own_sem.at[0]),
        pltpu.make_async_copy(wo, wo_all.at[pl.ds(pl.multiple_of(me * wo.shape[0], ROWS), wo.shape[0])], own_sem.at[1]),
        pltpu.make_async_copy(kv, kvs.at[pl.ds(blocks, blocks)], own_sem.at[2]),
    ]

    barrier = pltpu.get_barrier_semaphore()
    for step in range(1, n):
        pl.semaphore_signal(barrier, inc=1, device_id={"patch": lax.rem(me + step, n)}, device_id_type=MESH)
    pl.semaphore_signal(barrier, inc=1, device_id={"groups": mate}, device_id_type=MESH)
    pl.semaphore_signal(barrier, inc=1, device_id={"section": 1 - section}, device_id_type=MESH)
    pl.semaphore_wait(barrier, n + 1)

    flows = (
        (wq, wq_all, -1, half),
        (wq, wq_all, 1, half - 1),
        (wo, wo_all, -1, half - 1),
        (wo, wo_all, 1, half),
    )

    def remote(src, dst, send, recv, target):
        return pltpu.make_async_remote_copy(
            src_ref=src, dst_ref=dst, send_sem=send, recv_sem=recv,
            device_id=target, device_id_type=MESH,
        )

    def span(start, size):
        return pl.ds(pl.multiple_of(start, ROWS), size)

    def ring(flow, hop, received=False):
        own, every, way, _ = flows[flow]
        rows = own.shape[0]
        apart = exclusive_rows(rows)
        keep = rows - apart
        shard = at(place + way * (hop if received else hop - 1))
        dst = every.at[span(shard * rows + parity * apart, keep)]
        src = own.at[span(parity * apart, keep)] if hop == 1 and not received else dst
        target = {"patch": right if way < 0 else left}
        return remote(src, dst, ring_send.at[flow, hop - 1], ring_recv.at[flow, hop - 1], target)

    def across(flow, hop, received=False):
        own, every, way, _ = flows[flow]
        rows = own.shape[0]
        apart = exclusive_rows(rows)
        keep = rows - apart
        shard = at(place + way * hop)
        side = 1 - parity if received else parity
        ref = every.at[span(shard * rows + side * keep, apart)]
        return remote(ref, ref, mate_send.at[flow, hop - 1], mate_recv.at[flow, hop - 1], {"groups": mate})

    pair = me + 1 - 2 * odd
    onward, behind = me + 2 - 4 * odd, me - 2 + 4 * odd
    has_onward = (onward >= 0) & (onward < n)
    has_behind = (behind >= 0) & (behind < n)

    def rim(leg, block, received=False):
        near, far = 2 * (1 - odd) * blocks + block, 2 * odd * blocks + block
        if received:
            dst = kvs.at[far if leg else near]
        else:
            dst = kvs.at[far]
        src = kvs.at[near] if leg else kv.at[block]
        return remote(
            src, dst, rim_send.at[leg, block], rim_recv.at[leg, block],
            {"patch": onward if leg else pair},
        )

    def rim_forward(block):
        rim(0, block, True).wait_recv()
        pl.when(has_onward)(lambda: rim(1, block).start())

    few = chunks < n

    def scatter(step, received=False):
        peer = lax.rem(me + step, n)
        source = lax.rem(me + n - step, n)
        return remote(
            part.at[jnp.minimum(peer, chunks - 1) if few else peer], sums.at[source if received else me],
            text_send.at[step - 1], text_recv.at[step - 1], {"patch": peer},
        )

    def share(step, received=False):
        peer = lax.rem(me + step, n)
        slot = lax.rem(me + n - step, n) if received else me
        ref = text.at[span((jnp.minimum(slot, chunks - 1) if few else slot) * ROWS, ROWS)]
        return remote(ref, ref, share_send.at[step - 1], share_recv.at[step - 1], {"patch": peer})

    own_chunk = jnp.minimum(me, chunks - 1) if few else me
    own_sum = pltpu.make_async_copy(part.at[own_chunk], sums.at[me], text_sem.at[0])
    keep_sum = pltpu.make_async_copy(total, text.at[span(own_chunk * ROWS, ROWS)], text_sem.at[1])

    def text_start():
        when(few, me < chunks, own_sum.start)
        for step in range(1, n):
            when(few, lax.rem(me + step, n) < chunks, scatter(step).start)

    def text_reduce():
        def reduce():
            own_sum.wait()
            for step in range(1, n):
                scatter(step, True).wait_recv()
            total[...] = jnp.sum(sums[...].astype(jnp.float32), axis=0).astype(total.dtype)
            keep_sum.start()
            keep_sum.wait()
            for step in range(1, n):
                share(step).start()

        when(few, me < chunks, reduce)

    def text_arrive():
        for step in range(1, n):
            when(few, lax.rem(me + n - step, n) < chunks, share(step, True).wait_recv)

    def norm(source):
        step = ROWS

        @pl.loop(0, tokens // step)
        def _(index):
            window = pl.ds(pl.multiple_of(index * step, step), step)
            values = source[window, :].astype(jnp.float32)
            center = values - jnp.mean(values, axis=-1, keepdims=True)
            variance = jnp.mean(center * center, axis=-1, keepdims=True)
            scaled = center * lax.rsqrt(variance + EPSILON)
            normed[window, :] = (
                scaled * (1.0 + modulation[1:2, :]) + modulation[0:1, :]
            ).astype(normed.dtype)

    def project_query():
        @pl.loop(0, inner // TILE)
        def _(index):
            window = pl.ds(pl.multiple_of(index * TILE, TILE), TILE)
            query[:, window] = jnp.dot(
                normed[...], wq_all[:, window], preferred_element_type=jnp.float32
            ).astype(query.dtype)

    together = 4 if heads % 4 == 0 else 1

    def attend(first, last):
        bunches = heads // together

        @pl.loop(first * bunches, last * bunches)
        def _(index):
            block = lax.div(index, bunches)
            bunch = lax.rem(index, bunches)
            rows = pl.ds(pl.multiple_of(block * BLK, BLK), BLK)
            limit = lead + counts[block] * BLK
            live = lax.broadcasted_iota(jnp.int32, (BLK, keys), 1) < limit
            picks = [
                jnp.clip(chosen[block, slot] - (me - 1) * blocks, 0, 3 * blocks - 1)
                for slot in range(spread)
            ]
            for one in range(together):
                start = bunch * (together * HD) + one * HD
                columns = pl.ds(pl.multiple_of(start, HD), HD)
                beyond = pl.ds(pl.multiple_of(inner + start, HD), HD)
                key = jnp.concatenate([text[:, columns]] + [kvs[pick, :, columns] for pick in picks], axis=0)
                value = jnp.concatenate([text[:, beyond]] + [kvs[pick, :, beyond] for pick in picks], axis=0)
                scores = lax.dot_general(
                    query[rows, columns], key, (((1,), (1,)), ((), ())),
                    preferred_element_type=jnp.float32,
                )
                scores = jnp.where(live, scores, -1e30)
                peak = jnp.max(scores, axis=-1, keepdims=True)
                raised = jnp.exp((scores - peak) * HD ** (-0.5))
                whole = jnp.sum(raised, axis=-1, keepdims=True)
                share_of = jnp.dot(
                    raised.astype(jnp.bfloat16), value, preferred_element_type=jnp.float32
                )
                mixed[rows, columns] = (share_of / whole).astype(mixed.dtype)

    parts = width // (3 * TILE) if width % (3 * TILE) == 0 else 1
    part_width = width // parts

    def project_out(source, index_from, index_to):
        @pl.loop(index_from, index_to)
        def _(index):
            window = pl.ds(pl.multiple_of(index * TILE, TILE), TILE)
            projected = jnp.dot(mixed[...], wo_all[:, window], preferred_element_type=jnp.float32)
            out[:, window] = (
                source[:, window].astype(jnp.float32) + modulation[2:3, window] * projected
            ).astype(out.dtype)

    def hand(index):
        window = pl.ds(index * part_width, part_width)
        return remote(
            out.at[:, window], inbox.at[:, window],
            hand_send.at[index], hand_recv.at[index], {"section": 1 - section},
        )

    def relay(flow, hop):
        if hop <= flows[flow][3]:
            ring(flow, hop, True).wait_recv()
            if hop < flows[flow][3]:
                ring(flow, hop + 1).start()
            across(flow, hop).start()

    ring(0, 1).start()
    ring(1, 1).start()
    text_start()
    if LAG < 2:
        ring(2, 1).start()
        ring(3, 1).start()
    for copy in own_copies:
        copy.start()
    def rim_start():
        for block in range(blocks):
            rim(0, block).start()

    pl.when(section == 0)(rim_start)
    forwarded = 0
    pl.when(section == 0)(lambda: norm(state))
    for hop in range(1, half + 1):
        relay(0, hop)
        relay(1, hop)
        if hop == LAG - 1:
            ring(2, 1).start()
            ring(3, 1).start()
        if hop > LAG:
            relay(2, hop - LAG)
            relay(3, hop - LAG)
        if hop == max(half - 1, 1):
            text_reduce()
        if 2 <= hop and forwarded < blocks:
            pl.when(section == 0)(lambda: rim_forward(forwarded))
            forwarded += 1
    for block in range(forwarded, blocks):
        pl.when(section == 0)(lambda: rim_forward(block))
    pl.when(section == 1)(rim_start)

    def wait_query():
        for flow in range(2):
            for hop in range(1, flows[flow][3] + 1):
                across(flow, hop, True).wait_recv()
        own_copies[0].wait()

    def wait_keys():
        own_copies[2].wait()
        for block in range(blocks):
            pl.when(has_behind)(lambda: rim(1, block, True).wait_recv())
        text_arrive()

    todo = [h for h in range(half - LAG + 1, half + 1)]

    def relay_next():
        if todo:
            hop = todo.pop(0)
            relay(2, hop)
            relay(3, hop)

    wait_query()
    pl.when(section == 0)(project_query)
    relay_next()
    pl.when(section == 0)(wait_keys)
    for block in range(blocks):
        pl.when(section == 0)(lambda: attend(block, block + 1))
        relay_next()
    while todo:
        relay_next()
    @pl.when(section == 1)
    def _():
        for block in range(blocks):
            rim_forward(block)

    for flow in range(2, 4):
        for hop in range(1, flows[flow][3] + 1):
            across(flow, hop, True).wait_recv()
    own_copies[1].wait()

    each = part_width // TILE

    @pl.when(section == 0)
    def _():
        for index in range(parts):
            project_out(state, index * each, (index + 1) * each)
            if index:
                hand(index - 1).start()
        hand(parts - 1).start()

    @pl.when(section == 1)
    def _():
        for index in range(parts):
            hand(index).wait_recv()
        norm(inbox)
        project_query()
        wait_keys()
        attend(0, blocks)
        project_out(inbox, 0, width // TILE)

    for flow in range(4):
        for hop in range(1, flows[flow][3] + 1):
            across(flow, hop).wait_send()
            ring(flow, hop).wait_send()
    for step in range(1, n):
        when(few, lax.rem(me + step, n) < chunks, scatter(step).wait_send)
        when(few, me < chunks, share(step).wait_send)
    for block in range(blocks):
        rim(0, block).wait_send()
        pl.when(has_onward)(lambda: rim(1, block).wait_send())

    @pl.when(section == 0)
    def _():
        for index in range(parts):
            hand(index).wait_send()


def run(n, chosen, counts, modulation, state, wq, wo, kv, part):
    half = n // 2
    tokens, width = state.shape
    inner = wq.shape[1]
    blocks = kv.shape[0]
    smem = pl.BlockSpec(memory_space=pltpu.SMEM)
    vmem = pl.BlockSpec(memory_space=pltpu.VMEM)
    anywhere = pl.BlockSpec(memory_space=pl.ANY)
    dma = pltpu.SemaphoreType.DMA
    parts = width // (3 * TILE) if width % (3 * TILE) == 0 else 1
    b16 = jnp.bfloat16
    return pl.pallas_call(
        functools.partial(kernel, n),
        out_shape=jax.ShapeDtypeStruct(state.shape, state.dtype),
        in_specs=[smem, smem, vmem, vmem] + [anywhere] * 4,
        out_specs=vmem,
        scratch_shapes=[
            pltpu.VMEM((n * wq.shape[0], inner), b16),
            pltpu.VMEM((n * wo.shape[0], width), b16),
            pltpu.VMEM((3 * blocks,) + kv.shape[1:], b16),
            pltpu.VMEM((part.shape[0] * ROWS, kv.shape[2]), b16),
            pltpu.VMEM((n,) + part.shape[1:], part.dtype),
            pltpu.VMEM(part.shape[1:], b16),
            pltpu.VMEM((tokens, width), b16),
            pltpu.VMEM((tokens, inner), b16),
            pltpu.VMEM((tokens, inner), b16),
            pltpu.VMEM((tokens, width), b16),
            dma((4, half)), dma((4, half)), dma((4, half)), dma((4, half)),
            dma((2, blocks)), dma((2, blocks)),
            dma((n - 1,)), dma((n - 1,)), dma((n - 1,)), dma((n - 1,)),
            dma((parts,)), dma((parts,)), dma((3,)), dma((2,)),
        ],
        compiler_params=pltpu.CompilerParams(
            collective_id=0, has_side_effects=True, vmem_limit_bytes=60 * 2**20
        ),
        name="layers",
    )(chosen, counts, modulation, state, wq, wo, kv, part)


def local(
    hidden_in, text_rows, mod_table, timestep, w_query, w_out, w_text, stale_kv, mask_blocks, counts
):
    patch_id = lax.axis_index("patch")
    n = lax.axis_size("patch")
    width = text_rows.shape[1]
    modulation = lax.dynamic_index_in_dim(mod_table, timestep[0], 0, keepdims=False)[0]
    text_shift = lax.dynamic_slice_in_dim(modulation[3], patch_id * width, width, 0)
    text_scale = lax.dynamic_slice_in_dim(modulation[4], patch_id * width, width, 0)
    conditioned = (text_rows.astype(jnp.float32) * (1.0 + text_scale) + text_shift).astype(
        jnp.bfloat16
    )
    partial_pairs = jnp.dot(conditioned, w_text[0], preferred_element_type=jnp.float32)
    partial_pairs = partial_pairs.astype(jnp.bfloat16)
    kv = stale_kv[0].reshape(-1, BLK, stale_kv.shape[2])
    part = partial_pairs.reshape(-1, ROWS, partial_pairs.shape[1])
    result = run(n, mask_blocks, counts, modulation, hidden_in, w_query[0], w_out[0], kv, part)
    return result[None]


def solution(mesh):
    in_specs = (
        P(("groups", "patch"), None),
        P("groups", "patch"),
        P(None, "section", None, None),
        P("groups"),
        P("section", "patch", None),
        P("section", "patch", None),
        P("section", "patch", None),
        P("section", ("groups", "patch"), None),
        P(("groups", "patch"), None),
        P(("groups", "patch")),
    )
    out_specs = P("section", ("groups", "patch"), None)
    return jax.shard_map(local, mesh=mesh, in_specs=in_specs, out_specs=out_specs, check_vma=False)
```
